256 devices in a mesh: dp: 64 (over z, y, core), tensor: 4 (over x).
Axes of the slice: x: 4, y: 4, z: 8, core: 2. Of those that a mesh axis runs over, the one named last changes fastest.
Arguments:
- new_pages: bfloat16 [512, 128, 8192], P('dp', None, 'tensor'), may hold values from -6 to 6
- page_dest: int32 [512], replicated, may hold values from 0 to 511, as said below
- resident: bfloat16 [512, 128, 8192], P('dp', None, 'tensor'), may hold values from -6 to 6
- queries: bfloat16 [512, 4096], P('dp', 'tensor'), may hold values from -6 to 6
- page_table: int32 [512, 8], P('dp'), may hold values from 0 to 15, as said below
- cross_len: int32 [512], P('dp'), may hold values from 1 to 8, as said below
Outputs:
- arrived: bfloat16 [512, 128, 8192], P('dp', None, 'tensor')
- context: bfloat16 [512, 4096], P('dp', 'tensor')
The draws below stay inside these ranges and needn't reach their ends.
Inputs may be any that keep to these rules, and one draw needn't show every extreme that they name: page_dest is a permutation. There is one offset o, not zero and the same for all groups, such that every new page of group g (pages g * 8 to g * 8 + 7) goes to group g + o modulo the number of groups. `page_table`: the entries of one row are distinct slots of the request's group pool; the first entry is a resident slot; entries at or past the request's length are not read. `cross_len`: the first request of every group reads 8 pages.
All inputs are finite; a program needn't handle non-finite values.
Results may differ from the reference program's by a relative error of at most 0.0034.
Values may be sent and summed in bfloat16 or wider, within the bound.
A program may use at most 128 MiB of HBM per device.

```python
import jax
import jax.numpy as jnp
from jax import lax

D = 4096
HEADS = 16
HEAD_DIM = 256
PAGE = 128
MAXP = 8
REQ_DEV = 8
RES = 8
CAP = 8
KV = 8192
SLOTS = 16
PAGES = 512
REQS = 512
N_DP = 64


def draw_page_dest(key, part):
    offset = jax.random.randint(jax.random.fold_in(key, 41), (), 1, N_DP).astype(jnp.int32)
    group_keys = jax.random.split(jax.random.fold_in(key, 42), N_DP)
    slot_rows = jax.vmap(lambda k: jax.random.permutation(k, CAP))(group_keys).astype(jnp.int32)
    targets = (jnp.arange(N_DP, dtype=jnp.int32) + offset) % N_DP
    return (targets[:, None] * CAP + slot_rows).reshape(PAGES).astype(jnp.int32)


def draw_resident(key, part):
    shape = (N_DP * RES, PAGE, HEADS, 2, HEAD_DIM)
    base = jnp.clip(jax.random.normal(jax.random.fold_in(key, 1), shape, jnp.float32), -6.0, 6.0)
    return base.reshape(N_DP * RES, PAGE, KV).astype(jnp.bfloat16)


def draw_queries(key, part):
    shape = (REQS, HEADS, HEAD_DIM)
    base = jnp.clip(0.15 * jax.random.normal(jax.random.fold_in(key, 2), shape, jnp.float32), -6.0, 6.0)
    return base.reshape(REQS, D).astype(jnp.bfloat16)


def draw_page_table(key, part):
    first = jax.random.randint(jax.random.fold_in(key, 22), (REQS,), 0, RES).astype(jnp.int32)
    row_keys = jax.random.split(jax.random.fold_in(key, 21), REQS)
    others = jax.vmap(lambda k: jax.random.permutation(k, SLOTS - 1))(row_keys)[:, :MAXP - 1].astype(jnp.int32)
    others = others + (others >= first[:, None]).astype(jnp.int32)
    return jnp.concatenate([first[:, None], others], 1).astype(jnp.int32)


def draw_cross_len(key, part):
    lengths = jax.random.randint(jax.random.fold_in(key, 31), (REQS,), 1, MAXP + 1).astype(jnp.int32)
    return lengths.at[::REQ_DEV].set(MAXP).astype(jnp.int32)


def shard_levels(rng, dims, cuts, smallest, top_value):
    def one(axis_at, shards_of):
        steps = jax.random.uniform(jax.random.fold_in(jax.random.fold_in(rng, 6), axis_at), (shards_of,), jnp.float32, smallest / len(cuts), top_value / len(cuts))
        return jnp.repeat(jnp.exp(steps), dims[axis_at] // shards_of).reshape((-1,) + (1,) * (len(dims) - axis_at - 1))

    gain = one(*cuts[0])
    for cut in cuts[1:]:
        gain = gain * one(*cut)
    return gain


def gaussian(stream_key, shape, spread, limit, pieces=(), kind=jnp.bfloat16):
    values = spread * jax.random.normal(stream_key, shape, jnp.float32)
    if pieces:
        values = values * shard_levels(stream_key, shape, pieces, -0.22, 0.18)
    return jnp.clip(values, -limit, limit).astype(kind)


def setup_inputs(seed: int = 0) -> dict:
    keys = jax.random.split(jax.random.key(seed), 7)
    new_pages = gaussian(keys[0], (PAGES, PAGE, KV), 1.0, 6.0, ((0, 64), (2, 4)))
    page_dest = draw_page_dest(jax.random.fold_in(keys[6], 71), 0)
    resident = draw_resident(jax.random.fold_in(keys[6], 71), 0)
    queries = draw_queries(jax.random.fold_in(keys[6], 71), 0)
    page_table = draw_page_table(jax.random.fold_in(keys[6], 71), 0)
    cross_len = draw_cross_len(jax.random.fold_in(keys[6], 71), 0)
    return dict(new_pages=new_pages, page_dest=page_dest, resident=resident, queries=queries, page_table=page_table, cross_len=cross_len)


def attend_group(items):
    res_pages, new_slots, query_rows, table_rows, length_rows = items
    pool = jnp.concatenate([res_pages, new_slots], 0).astype(jnp.float32)
    pool = pool.reshape(SLOTS, PAGE, HEADS, 2, HEAD_DIM)
    within = jnp.arange(MAXP, dtype=jnp.int32)[None, :] < length_rows[:, None]
    member = (table_rows[:, :, None] == jnp.arange(SLOTS, dtype=jnp.int32)[None, None, :]) & within[:, :, None]
    live = jnp.any(member, axis=1)
    scores = jnp.einsum("rhd,sphd->rhsp", query_rows.astype(jnp.float32), pool[:, :, :, 0, :], precision=lax.Precision.HIGHEST)
    scores = jnp.where(live[:, None, :, None], scores, -jnp.inf)
    peak = jnp.max(scores, axis=(2, 3), keepdims=True)
    prob = jnp.exp(scores - peak)
    total = jnp.sum(prob, axis=(2, 3))
    weights = lax.optimization_barrier(prob.astype(jnp.bfloat16)).astype(jnp.float32)
    summed = jnp.einsum("rhsp,sphd->rhd", weights, pool[:, :, :, 1, :], precision=lax.Precision.HIGHEST)
    return (summed / total[:, :, None]).astype(jnp.bfloat16).reshape(REQ_DEV, D)


def reference(new_pages, page_dest, resident, queries, page_table, cross_len):
    arrived = jnp.zeros((PAGES, PAGE, KV), jnp.bfloat16).at[page_dest].set(new_pages)
    groups = (
        resident.reshape(N_DP, RES, PAGE, KV),
        arrived.reshape(N_DP, CAP, PAGE, KV),
        queries.reshape(N_DP, REQ_DEV, HEADS, HEAD_DIM),
        page_table.reshape(N_DP, REQ_DEV, MAXP),
        cross_len.reshape(N_DP, REQ_DEV),
    )
    context = lax.map(attend_group, groups)
    return arrived, context.reshape(REQS, D)
```

```python
import jax
import jax.numpy as jnp
from jax import lax
from jax.experimental import pallas as pl
from jax.experimental.pallas import tpu as pltpu
from jax.sharding import PartitionSpec as P

MESH = pl.DeviceIdType.MESH
HEAD_DIM = 256
CHUNKS = 2
UNITS = 16

ROUTES = (
    ((16, ((0, 0, 0), (1, 0, 1),)),),
    ((4, ((0, 0, 0), (6, 0, 0), (4, 0, 1), (2, 0, 1),)), (12, ((0, 0, 0), (2, 0, 1),)),),
    ((3, ((0, 0, 0), (6, 0, 0), (4, 0, 1), (3, 0, 1),)), (13, ((0, 0, 0), (3, 0, 1),)),),
    ((16, ((0, 0, 0), (4, 0, 1),)),),
    ((1, ((0, 0, 0), (2, -3, 1), (4, -6, 1), (5, -8, 1),)), (15, ((0, 0, 0), (5, 0, 1),)),),
    ((2, ((0, 0, 0), (2, 0, 0), (4, 0, 1), (6, 0, 1),)), (3, ((0, 0, 0), (5, 0, 0), (6, 0, 1),)), (3, ((0, 0, 0), (1, 0, 1), (6, 0, 1),)), (8, ((0, 0, 0), (6, 0, 1),)),),
    ((1, ((0, 0, 0), (0, -3, 0), (0, -6, 1), (7, -8, 1),)), (15, ((0, 0, 0), (7, 0, 1),)),),
    ((2, ((0, 0, 0), (0, -3, 0), (4, -6, 0), (0, -7, 0),)), (14, ((0, 0, 0), (0, 1, 0),)),),
    ((4, ((0, 0, 0), (3, 0, 0), (3, 1, 1), (1, 1, 1),)), (5, ((0, 0, 0), (6, 0, 0), (6, 1, 1), (1, 1, 1),)), (2, ((0, 0, 0), (0, -3, 0), (2, -4, 1), (1, -7, 1),)), (5, ((0, 0, 0), (1, 1, 1),)),),
    ((3, ((0, 0, 0), (6, 0, 0), (6, 1, 1), (2, 1, 1),)), (3, ((0, 0, 0), (4, 0, 0), (4, 1, 1), (2, 1, 1),)), (2, ((0, 0, 0), (1, -3, 0), (1, -6, 1), (2, -7, 1),)), (4, ((0, 0, 0), (0, 1, 1), (2, 1, 1),)), (4, ((0, 0, 0), (2, 0, 0), (2, 1, 1),)),),
    ((2, ((0, 0, 0), (6, -3, 0), (6, -6, 1), (3, -7, 1),)), (2, ((0, 0, 0), (6, 0, 0), (6, 1, 1), (3, 1, 1),)), (6, ((0, 0, 0), (0, 1, 1), (3, 1, 1),)), (6, ((0, 0, 0), (3, 0, 0), (3, 1, 1),)),),
    ((2, ((0, 0, 0), (0, -3, 1), (1, -6, 1), (4, -7, 1),)), (1, ((0, 0, 0), (2, -3, 0), (4, -5, 0), (4, -7, 1),)), (7, ((0, 0, 0), (0, 1, 1), (4, 1, 1),)), (6, ((0, 0, 0), (4, 0, 0), (4, 1, 1),)),),
    ((3, ((0, 0, 0), (3, -3, 0), (3, -6, 1), (5, -7, 1),)), (2, ((0, 0, 0), (2, 0, 0), (2, 1, 1), (5, 1, 1),)), (5, ((0, 0, 0), (0, 1, 1), (5, 1, 1),)), (6, ((0, 0, 0), (5, 0, 0), (5, 1, 1),)),),
    ((3, ((0, 0, 0), (1, -3, 0), (1, -6, 1), (6, -7, 1),)), (3, ((0, 0, 0), (2, 0, 0), (2, 1, 1), (6, 1, 1),)), (3, ((0, 0, 0), (4, 0, 0), (4, 1, 1), (6, 1, 1),)), (4, ((0, 0, 0), (6, 0, 0), (6, 1, 1),)), (3, ((0, 0, 0), (0, 1, 1), (6, 1, 1),)),),
    ((2, ((0, 0, 0), (0, -3, 0), (7, -5, 0), (7, -7, 1),)), (2, ((0, 0, 0), (5, -3, 0), (5, -6, 1), (7, -7, 1),)), (12, ((0, 0, 0), (7, 1, 1),)),),
    ((4, ((0, 0, 0), (2, -3, 0), (0, -6, 0),)), (12, ((0, 0, 0), (0, 2, 0),)),),
    ((4, ((0, 0, 0), (5, 0, 0), (5, 1, 1), (1, 2, 1),)), (4, ((0, 0, 0), (1, -3, 0), (1, -6, 1),)), (4, ((0, 0, 0), (4, 0, 0), (1, 2, 1),)), (4, ((0, 0, 0), (7, 0, 1), (1, 2, 1),)),),
    ((3, ((0, 0, 0), (4, 0, 0), (4, 1, 1), (2, 2, 1),)), (3, ((0, 0, 0), (6, 0, 0), (6, 1, 1), (2, 2, 1),)), (3, ((0, 0, 0), (0, 1, 1), (2, 2, 1),)), (3, ((0, 0, 0), (2, 0, 0), (2, 2, 1),)), (4, ((0, 0, 0), (0, -3, 1), (2, -6, 1),)),),
    ((3, ((0, 0, 0), (0, -3, 1), (3, -6, 1),)), (6, ((0, 0, 0), (0, 1, 1), (3, 2, 1),)), (5, ((0, 0, 0), (3, 0, 0), (3, 2, 1),)), (2, ((0, 0, 0), (3, -3, 0), (3, -6, 1),)),),
    ((3, ((0, 0, 0), (0, -3, 1), (4, -6, 1),)), (2, ((0, 0, 0), (4, -3, 0), (4, -6, 1),)), (6, ((0, 0, 0), (4, 0, 0), (4, 2, 1),)), (5, ((0, 0, 0), (0, 1, 1), (4, 2, 1),)),),
    ((2, ((0, 0, 0), (3, 0, 0), (3, 1, 1), (5, 2, 1),)), (4, ((0, 0, 0), (5, 0, 0), (5, 2, 1),)), (5, ((0, 0, 0), (0, 1, 1), (5, 2, 1),)), (3, ((0, 0, 0), (5, -3, 0), (5, -6, 1),)), (2, ((0, 0, 0), (0, -3, 1), (5, -6, 1),)),),
    ((6, ((0, 0, 0), (1, 0, 0), (1, 1, 1), (6, 2, 1),)), (5, ((0, 0, 0), (5, 0, 0), (5, 1, 1), (6, 2, 1),)), (5, ((0, 0, 0), (0, -3, 1), (6, -6, 1),)),),
    ((3, ((0, 0, 0), (0, -3, 1), (7, -6, 1),)), (3, ((0, 0, 0), (7, -3, 0), (7, -6, 1),)), (10, ((0, 0, 0), (7, 2, 1),)),),
    ((6, ((0, 0, 0), (2, -3, 0), (0, -5, 0),)), (10, ((0, 0, 0), (0, 3, 0),)),),
    ((6, ((0, 0, 0), (0, -3, 1), (1, -5, 1),)), (5, ((0, 0, 0), (4, 2, 1), (1, 3, 1),)), (5, ((0, 0, 0), (4, 3, 0), (1, 3, 1),)),),
    ((5, ((0, 0, 0), (3, 0, 0), (3, 1, 1), (2, 3, 1),)), (5, ((0, 0, 0), (7, 2, 0), (7, 3, 1), (2, 3, 1),)), (6, ((0, 0, 0), (3, -3, 0), (2, -5, 1),)),),
    ((4, ((0, 0, 0), (0, 1, 1), (3, 3, 1),)), (4, ((0, 0, 0), (0, -3, 1), (3, -5, 1),)), (3, ((0, 0, 0), (3, -3, 0), (3, -5, 1),)), (5, ((0, 0, 0), (3, 2, 0), (3, 3, 1),)),),
    ((5, ((0, 0, 0), (4, 1, 0), (4, 3, 1),)), (4, ((0, 0, 0), (0, 1, 1), (4, 3, 1),)), (4, ((0, 0, 0), (0, -3, 1), (4, -5, 1),)), (3, ((0, 0, 0), (4, -3, 0), (4, -5, 1),)),),
    ((2, ((0, 0, 0), (3, 0, 0), (3, 1, 1), (5, 3, 1),)), (4, ((0, 0, 0), (0, -3, 1), (5, -5, 1),)), (4, ((0, 0, 0), (0, 1, 1), (5, 3, 1),)), (3, ((0, 0, 0), (5, 1, 0), (5, 3, 1),)), (3, ((0, 0, 0), (5, -3, 0), (5, -5, 1),)),),
    ((4, ((0, 0, 0), (5, -3, 0), (5, -5, 1), (6, -5, 1),)), (4, ((0, 0, 0), (1, -1, 0), (1, -4, 1), (6, -5, 1),)), (8, ((0, 0, 0), (3, 0, 1), (6, 3, 1),)),),
    ((8, ((0, 0, 0), (5, 1, 0), (7, 3, 1),)), (4, ((0, 0, 0), (4, -3, 0), (7, -5, 1),)), (4, ((0, 0, 0), (0, -3, 1), (7, -5, 1),)),),
    ((8, ((0, 0, 0), (2, -3, 0), (0, -4, 0),)), (8, ((0, 0, 0), (2, 1, 0), (0, 4, 0),)),),
    ((4, ((0, 0, 0), (2, 2, 0), (1, 4, 1),)), (8, ((0, 0, 0), (3, -3, 0), (1, -4, 1),)), (4, ((0, 0, 0), (3, 2, 1), (1, 4, 1),)),),
    ((4, ((0, 0, 0), (3, 0, 0), (3, 1, 1), (2, 4, 1),)), (4, ((0, 0, 0), (7, 0, 0), (7, 1, 1), (2, 4, 1),)), (8, ((0, 0, 0), (3, -3, 0), (2, -4, 1),)),),
    ((2, ((0, 0, 0), (6, -2, 0), (6, -4, 1), (3, -4, 1),)), (4, ((0, 0, 0), (0, 1, 1), (3, 4, 1),)), (3, ((0, 0, 0), (3, 2, 0), (3, 4, 1),)), (4, ((0, 0, 0), (3, -2, 0), (3, -4, 1),)), (3, ((0, 0, 0), (0, -3, 1), (3, -4, 1),)),),
    ((4, ((0, 0, 0), (0, 1, 1), (4, 4, 1),)), (3, ((0, 0, 0), (4, 2, 0), (4, 4, 1),)), (5, ((0, 0, 0), (4, -2, 0), (4, -4, 1),)), (4, ((0, 0, 0), (0, -3, 1), (4, -4, 1),)),),
    ((6, ((0, 0, 0), (5, -2, 0), (5, -4, 1),)), (3, ((0, 0, 0), (0, -3, 1), (5, -4, 1),)), (4, ((0, 0, 0), (0, 1, 1), (5, 4, 1),)), (3, ((0, 0, 0), (5, 2, 0), (5, 4, 1),)),),
    ((5, ((0, 0, 0), (5, -2, 0), (5, -4, 1), (6, -4, 1),)), (5, ((0, 0, 0), (1, -2, 0), (1, -4, 1), (6, -4, 1),)), (6, ((0, 0, 0), (5, 1, 1), (6, 4, 1),)),),
    ((6, ((0, 0, 0), (1, 1, 1), (7, 4, 1),)), (5, ((0, 0, 0), (3, -2, 1), (7, -4, 1),)), (5, ((0, 0, 0), (4, -3, 0), (7, -4, 1),)),),
    ((6, ((0, 0, 0), (2, 2, 0), (0, 5, 0),)), (10, ((0, 0, 0), (0, -3, 0),)),),
    ((3, ((0, 0, 0), (4, 2, 1), (1, 5, 1),)), (3, ((0, 0, 0), (6, 3, 0), (1, 5, 1),)), (10, ((0, 0, 0), (1, -3, 1),)),),
    ((6, ((0, 0, 0), (3, -1, 0), (3, -3, 1), (2, -3, 1),)), (5, ((0, 0, 0), (7, 0, 0), (7, -2, 1), (2, -3, 1),)), (5, ((0, 0, 0), (4, 3, 0), (2, 5, 1),)),),
    ((2, ((0, 0, 0), (5, -1, 0), (5, -3, 1), (3, -3, 1),)), (5, ((0, 0, 0), (0, -3, 1), (3, -3, 1),)), (3, ((0, 0, 0), (3, 3, 0), (3, 5, 1),)), (2, ((0, 0, 0), (0, 2, 1), (3, 5, 1),)), (4, ((0, 0, 0), (3, -1, 0), (3, -3, 1),)),),
    ((3, ((0, 0, 0), (4, 3, 0), (4, 5, 1),)), (2, ((0, 0, 0), (0, 2, 1), (4, 5, 1),)), (6, ((0, 0, 0), (0, -3, 1), (4, -3, 1),)), (5, ((0, 0, 0), (4, -1, 0), (4, -3, 1),)),),
    ((6, ((0, 0, 0), (0, -3, 1), (5, -3, 1),)), (5, ((0, 0, 0), (5, -1, 0), (5, -3, 1),)), (2, ((0, 0, 0), (5, 3, 0), (5, 5, 1),)), (3, ((0, 0, 0), (0, 2, 1), (5, 5, 1),)),),
    ((6, ((0, 0, 0), (1, -1, 0), (1, -3, 1), (6, -3, 1),)), (6, ((0, 0, 0), (5, -1, 0), (5, -3, 1), (6, -3, 1),)), (4, ((0, 0, 0), (4, 3, 0), (6, 5, 1),)),),
    ((4, ((0, 0, 0), (6, -2, 0), (4, -3, 1), (7, -3, 1),)), (4, ((0, 0, 0), (1, -3, 1), (7, -3, 1),)), (4, ((0, 0, 0), (6, 3, 0), (7, 5, 1),)), (4, ((0, 0, 0), (5, -2, 0), (7, -3, 1),)),),
    ((4, ((0, 0, 0), (2, 3, 0), (0, 6, 0),)), (12, ((0, 0, 0), (0, -2, 0),)),),
    ((2, ((0, 0, 0), (0, 1, 0), (6, 3, 1), (1, 6, 1),)), (2, ((0, 0, 0), (0, 3, 0), (5, 6, 0), (1, 6, 1),)), (12, ((0, 0, 0), (1, -2, 1),)),),
    ((3, ((0, 0, 0), (2, -1, 0), (4, -2, 1), (2, -2, 1),)), (3, ((0, 0, 0), (6, 0, 0), (6, -2, 1), (2, -2, 1),)), (3, ((0, 0, 0), (7, 1, 0), (7, 3, 1), (2, 6, 1),)), (4, ((0, 0, 0), (0, -2, 1), (2, -2, 1),)), (3, ((0, 0, 0), (4, -1, 0), (2, -2, 1),)),),
    ((2, ((0, 0, 0), (5, 0, 0), (5, -2, 1), (3, -2, 1),)), (3, ((0, 0, 0), (0, 1, 0), (3, 4, 0), (3, 6, 1),)), (5, ((0, 0, 0), (3, 0, 0), (3, -2, 1),)), (6, ((0, 0, 0), (0, -2, 1), (3, -2, 1),)),),
    ((2, ((0, 0, 0), (0, 1, 1), (6, 3, 1), (4, 6, 1),)), (1, ((0, 0, 0), (6, 1, 0), (4, 4, 0), (4, 6, 1),)), (7, ((0, 0, 0), (4, 0, 0), (4, -2, 1),)), (6, ((0, 0, 0), (0, -2, 1), (4, -2, 1),)),),
    ((2, ((0, 0, 0), (2, 0, 0), (2, -2, 1), (5, -2, 1),)), (2, ((0, 0, 0), (6, 1, 0), (5, 4, 0), (5, 6, 1),)), (6, ((0, 0, 0), (5, 0, 0), (5, -2, 1),)), (6, ((0, 0, 0), (0, -2, 1), (5, -2, 1),)),),
    ((2, ((0, 0, 0), (7, 1, 0), (7, 3, 1), (6, 6, 1),)), (3, ((0, 0, 0), (2, 0, 0), (2, -2, 1), (6, -2, 1),)), (3, ((0, 0, 0), (4, 0, 0), (4, -2, 1), (6, -2, 1),)), (4, ((0, 0, 0), (0, -2, 1), (6, -2, 1),)), (4, ((0, 0, 0), (6, 0, 0), (6, -2, 1),)),),
    ((4, ((0, 0, 0), (5, 0, 0), (5, -2, 1), (7, -2, 1),)), (2, ((0, 0, 0), (3, 2, 0), (7, 5, 0), (7, 6, 1),)), (5, ((0, 0, 0), (6, -1, 0), (7, -2, 1),)), (5, ((0, 0, 0), (0, -2, 1), (7, -2, 1),)),),
    ((2, ((0, 0, 0), (0, 1, 0), (3, 4, 0), (0, 7, 0),)), (14, ((0, 0, 0), (0, -1, 0),)),),
    ((1, ((0, 0, 0), (0, 1, 1), (0, 4, 1), (1, 7, 1),)), (15, ((0, 0, 0), (1, -1, 1),)),),
    ((2, ((0, 0, 0), (6, 0, 0), (4, -1, 1), (2, -1, 1),)), (4, ((0, 0, 0), (3, 0, 0), (2, -1, 1),)), (4, ((0, 0, 0), (7, -1, 1), (2, -1, 1),)), (6, ((0, 0, 0), (2, -1, 1),)),),
    ((1, ((0, 0, 0), (6, 2, 0), (4, 4, 1), (3, 7, 1),)), (15, ((0, 0, 0), (3, -1, 1),)),),
    ((16, ((0, 0, 0), (4, -1, 1),)),),
    ((3, ((0, 0, 0), (2, 0, 0), (4, -1, 1), (5, -1, 1),)), (13, ((0, 0, 0), (5, -1, 1),)),),
    ((4, ((0, 0, 0), (2, 0, 0), (4, -1, 1), (6, -1, 1),)), (12, ((0, 0, 0), (6, -1, 1),)),),
    ((16, ((0, 0, 0), (7, -1, 1),)),),
)


def hop(at, start, end, turn):
    (e0, b0, k0), (e1, b1, k1) = start, end
    source = lax.rem(lax.rem(at, 8) - e0 + 8, 8)
    carry = lax.div(source + turn, 8)
    z = lax.rem(lax.div(at, 8) + (b1 - b0 + 64) + (k1 - k0) * carry, 8)
    return z * 8 + lax.rem(source + e1, 8)


def handoff(pages, offset):
    turn = offset % 8
    rows = pages.shape[0]
    paths = []
    row = 0
    for units, states in ROUTES[offset - 1]:
        size = units * rows // (UNITS * CHUNKS)
        paths.append((row, size, states))
        row += size * CHUNKS
    legs = {}
    for p, (_, _, states) in enumerate(paths):
        for i in range(len(states) - 1):
            legs[p, i] = len(legs)
    depth = max(len(states) for _, _, states in paths) - 1
    moves = sorted({m for _, _, states in paths for m in zip(states, states[1:])})

    inner = {}
    for p, i in legs:
        if (p, i + 1) in legs:
            inner[p, i] = len(inner) * CHUNKS
    sent = sum(paths[p][1] * CHUNKS for p, _ in legs)
    held = max(sent, depth * rows)

    def kernel(src, dst, relay, send_sem, last_sem, inner_sem):
        me = lax.axis_index("dp")
        column = lax.axis_index("tensor")
        to = {m: hop(me, *m, turn) for m in moves}

        def copy(p, i, j):
            first, size, states = paths[p]
            span = pl.ds(pl.multiple_of(first + j * size, 8), size)
            before = pl.ds(pl.multiple_of((i - 1) * rows + first + j * size, 8), size)
            after = pl.ds(pl.multiple_of(i * rows + first + j * size, 8), size)
            return pltpu.make_async_remote_copy(
                src_ref=src.at[span] if i == 0 else relay.at[before],
                dst_ref=relay.at[after] if (p, i) in inner else dst.at[span],
                send_sem=send_sem,
                recv_sem=inner_sem.at[inner[p, i] + j] if (p, i) in inner else last_sem,
                device_id=(to[states[i], states[i + 1]], column),
                device_id_type=MESH,
            )

        @pl.loop(0, CHUNKS)
        def _(j):
            for p in range(len(paths)):
                copy(p, 0, j).start()

        if depth > 1:

            @pl.loop(0, CHUNKS + depth - 2)
            def _(step):
                for i in range(1, depth):
                    j = step - (i - 1)

                    @pl.when((j >= 0) & (j < CHUNKS))
                    def _():
                        for p in range(len(paths)):
                            if (p, i) in legs:
                                copy(p, i - 1, j).wait_recv()
                                copy(p, i, j).start()

        pltpu.make_async_copy(dst, dst, last_sem).wait()
        everything = relay.at[pl.ds(0, sent)]
        pltpu.make_async_copy(everything, everything, send_sem).wait()

    return pl.pallas_call(
        kernel,
        out_shape=jax.ShapeDtypeStruct(pages.shape, pages.dtype),
        in_specs=[pl.BlockSpec(memory_space=pl.ANY)],
        out_specs=pl.BlockSpec(memory_space=pl.ANY),
        scratch_shapes=[
            pltpu.VMEM((held, pages.shape[1]), pages.dtype),
            pltpu.SemaphoreType.DMA,
            pltpu.SemaphoreType.DMA,
            pltpu.SemaphoreType.DMA((max(len(inner), 1) * CHUNKS,)),
        ],
        compiler_params=pltpu.CompilerParams(has_side_effects=True, vmem_limit_bytes=32 << 20),
        name=f"handoff{offset}",
    )(pages)


def attend(moved, resident, queries, page_dest, page_table, cross_len):
    cap, page, width = moved.shape
    n_res = resident.shape[0]
    n_slots = n_res + cap
    requests = queries.shape[0]
    heads = width // (2 * HEAD_DIM)
    groups = page_dest.shape[0] // cap

    def kernel(dest, length, moved, resident, queries, table, arrived, context, pool, scores, in_sem, out_sem):
        offset = dest[0] // cap
        maker = (lax.axis_index("dp") - offset + groups) % groups

        def fetch(s):
            src = resident.at[s] if s < n_res else moved.at[s - n_res]
            return pltpu.make_async_copy(src, pool.at[s], in_sem.at[s])

        def slot(q):
            return dest[maker * cap + q] % cap

        def place(q):
            return pltpu.make_async_copy(pool.at[n_res + q], arrived.at[slot(q)], out_sem.at[q])

        for s in range(n_slots):
            fetch(s).start()
        row = lax.broadcasted_iota(jnp.int32, table.shape, 0)
        limit = jnp.zeros(table.shape, jnp.int32)
        for r in range(requests):
            limit = jnp.where(row == r, length[r], limit)
        within = lax.broadcasted_iota(jnp.int32, table.shape, 1) < limit
        entries = jnp.where(within, table[...], -1)
        for s in range(n_slots):
            fetch(s).wait()
            if s >= n_res:
                place(s - n_res).start()
            where = s if s < n_res else n_res + slot(s - n_res)
            live = jnp.max((entries == where).astype(jnp.int32), axis=1, keepdims=True) > 0
            for h in range(heads):
                keys = pool[s, :, 2 * h * HEAD_DIM : (2 * h + 1) * HEAD_DIM]
                part = lax.dot_general(
                    queries[:, h * HEAD_DIM : (h + 1) * HEAD_DIM],
                    keys,
                    (((1,), (1,)), ((), ())),
                    preferred_element_type=jnp.float32,
                )
                scores[h, :, s * page : (s + 1) * page] = jnp.where(live, part, -jnp.inf)
        for h in range(heads):
            s = scores[h]
            prob = jnp.exp(s - jnp.max(s, axis=1, keepdims=True))
            total = jnp.sum(prob, axis=1, keepdims=True)
            weights = prob.astype(jnp.bfloat16)
            values = pool[:, :, (2 * h + 1) * HEAD_DIM : (2 * h + 2) * HEAD_DIM]
            summed = jnp.dot(
                weights, values.reshape(n_slots * page, HEAD_DIM), preferred_element_type=jnp.float32
            )
            context[:, h * HEAD_DIM : (h + 1) * HEAD_DIM] = (summed / total).astype(context.dtype)
        for q in range(cap):
            place(q).wait()

    vmem = pl.BlockSpec(memory_space=pltpu.VMEM)
    hbm = pl.BlockSpec(memory_space=pl.ANY)
    return pl.pallas_call(
        kernel,
        grid_spec=pltpu.PrefetchScalarGridSpec(
            num_scalar_prefetch=2,
            grid=(),
            in_specs=[hbm, hbm, vmem, vmem],
            out_specs=[hbm, vmem],
            scratch_shapes=[
                pltpu.VMEM((n_slots, page, width), moved.dtype),
                pltpu.VMEM((heads, requests, n_slots * page), jnp.float32),
                pltpu.SemaphoreType.DMA((n_slots,)),
                pltpu.SemaphoreType.DMA((cap,)),
            ],
        ),
        out_shape=[
            jax.ShapeDtypeStruct(moved.shape, moved.dtype),
            jax.ShapeDtypeStruct(queries.shape, queries.dtype),
        ],
        compiler_params=pltpu.CompilerParams(vmem_limit_bytes=60 << 20),
        name="attend",
    )(page_dest, cross_len, moved, resident, queries, page_table)


def local(new_pages, page_dest, resident, queries, page_table, cross_len):
    cap, page, width = new_pages.shape
    groups = lax.axis_size("dp")
    offset = lax.shift_right_logical(page_dest[0], cap.bit_length() - 1)
    per_z = 8

    def from_z(a):
        def pick(x):
            first = 1 if a == 0 else 0
            ways = [lambda y, o=a * per_z + r: handoff(y, o) for r in range(first, per_z)]
            return lax.switch((offset & (per_z - 1)) - first, ways, x)

        return pick

    moved = lax.switch(
        lax.shift_right_logical(offset, 3),
        [from_z(a) for a in range(groups // per_z)],
        new_pages.reshape(cap * page, width),
    )
    return tuple(
        attend(moved.reshape(cap, page, width), resident, queries, page_dest, page_table, cross_len)
    )


def solution(mesh):
    return jax.shard_map(
        local,
        mesh=mesh,
        in_specs=(
            P("dp", None, "tensor"),
            P(),
            P("dp", None, "tensor"),
            P("dp", "tensor"),
            P("dp", None),
            P("dp"),
        ),
        out_specs=(P("dp", None, "tensor"), P("dp", "tensor")),
        check_vma=False,
    )
```

```python
import jax
import jax.numpy as jnp
from jax import lax
from jax.experimental import pallas as pl
from jax.experimental.pallas import tpu as pltpu
from jax.sharding import PartitionSpec as P

MESH = pl.DeviceIdType.MESH
HEAD_DIM = 256
CHUNKS = 2
UNITS = 32

ROUTES = (
    ((32, ((0, 0, 0), (1, 0, 1),)),),
    ((8, ((0, 0, 0), (6, 0, 0), (4, 0, 1), (2, 0, 1),)), (24, ((0, 0, 0), (2, 0, 1),)),),
    ((3, ((0, 0, 0), (0, -3, 0), (3, -6, 0), (3, -8, 1),)), (5, ((0, 0, 0), (6, 0, 0), (4, 0, 1), (3, 0, 1),)), (24, ((0, 0, 0), (3, 0, 1),)),),
    ((32, ((0, 0, 0), (4, 0, 1),)),),
    ((3, ((0, 0, 0), (2, -3, 1), (4, -5, 1), (5, -8, 1),)), (29, ((0, 0, 0), (5, 0, 1),)),),
    ((3, ((0, 0, 0), (2, 0, 0), (4, 0, 1), (6, 0, 1),)), (3, ((0, 0, 0), (0, -3, 0), (6, -6, 0), (6, -8, 1),)), (3, ((0, 0, 0), (2, 0, 1), (4, 0, 1), (6, 0, 1),)), (6, ((0, 0, 0), (5, 0, 0), (6, 0, 1),)), (17, ((0, 0, 0), (7, 0, 1), (6, 0, 1),)),),
    ((3, ((0, 0, 0), (6, -3, 0), (6, -5, 0), (7, -8, 1),)), (29, ((0, 0, 0), (7, 0, 1),)),),
    ((4, ((0, 0, 0), (0, -3, 0), (4, -6, 0), (0, -7, 0),)), (28, ((0, 0, 0), (0, 1, 0),)),),
    ((7, ((0, 0, 0), (3, 0, 0), (3, 1, 1), (1, 1, 1),)), (7, ((0, 0, 0), (6, 0, 0), (6, 1, 1), (1, 1, 1),)), (4, ((0, 0, 0), (3, -3, 0), (1, -5, 0), (1, -7, 1),)), (7, ((0, 0, 0), (1, 0, 0), (1, 1, 1),)), (7, ((0, 0, 0), (7, 0, 1), (1, 1, 1),)),),
    ((5, ((0, 0, 0), (1, -3, 0), (1, -6, 1), (2, -7, 1),)), (11, ((0, 0, 0), (5, 0, 0), (5, 1, 1), (2, 1, 1),)), (8, ((0, 0, 0), (0, 1, 1), (2, 1, 1),)), (8, ((0, 0, 0), (2, 0, 0), (2, 1, 1),)),),
    ((5, ((0, 0, 0), (0, -3, 1), (5, -6, 1), (3, -7, 1),)), (5, ((0, 0, 0), (6, 0, 0), (6, 1, 1), (3, 1, 1),)), (11, ((0, 0, 0), (0, 1, 1), (3, 1, 1),)), (11, ((0, 0, 0), (3, 0, 0), (3, 1, 1),)),),
    ((3, ((0, 0, 0), (0, -3, 1), (1, -6, 1), (4, -7, 1),)), (3, ((0, 0, 0), (2, -3, 0), (4, -5, 0), (4, -7, 1),)), (13, ((0, 0, 0), (0, 1, 1), (4, 1, 1),)), (13, ((0, 0, 0), (4, 0, 0), (4, 1, 1),)),),
    ((6, ((0, 0, 0), (6, -3, 0), (6, -6, 1), (5, -7, 1),)), (3, ((0, 0, 0), (2, 0, 0), (2, 1, 1), (5, 1, 1),)), (3, ((0, 0, 0), (3, 0, 0), (3, 1, 1), (5, 1, 1),)), (10, ((0, 0, 0), (0, 1, 1), (5, 1, 1),)), (10, ((0, 0, 0), (5, 0, 0), (5, 1, 1),)),),
    ((2, ((0, 0, 0), (4, -3, 0), (4, -6, 1), (6, -7, 1),)), (5, ((0, 0, 0), (1, -3, 0), (1, -6, 1), (6, -7, 1),)), (6, ((0, 0, 0), (2, 0, 0), (2, 1, 1), (6, 1, 1),)), (6, ((0, 0, 0), (4, 0, 0), (4, 1, 1), (6, 1, 1),)), (7, ((0, 0, 0), (6, 0, 0), (6, 1, 1),)), (6, ((0, 0, 0), (0, 1, 1), (6, 1, 1),)),),
    ((7, ((0, 0, 0), (0, -2, 0), (7, -4, 0), (7, -7, 1),)), (25, ((0, 0, 0), (7, 1, 1),)),),
    ((8, ((0, 0, 0), (2, -3, 0), (0, -6, 0),)), (24, ((0, 0, 0), (0, 2, 0),)),),
    ((8, ((0, 0, 0), (5, 0, 0), (5, 1, 1), (1, 2, 1),)), (8, ((0, 0, 0), (1, -3, 0), (1, -6, 1),)), (8, ((0, 0, 0), (7, 0, 1), (1, 2, 1),)), (8, ((0, 0, 0), (2, 1, 0), (1, 2, 1),)),),
    ((15, ((0, 0, 0), (5, 0, 0), (5, 1, 1), (2, 2, 1),)), (9, ((0, 0, 0), (2, -3, 0), (2, -6, 1),)), (8, ((0, 0, 0), (2, 2, 1),)),),
    ((5, ((0, 0, 0), (6, 0, 0), (6, 1, 1), (3, 2, 1),)), (9, ((0, 0, 0), (0, 1, 1), (3, 2, 1),)), (9, ((0, 0, 0), (3, 0, 0), (3, 2, 1),)), (9, ((0, 0, 0), (6, -3, 1), (3, -6, 1),)),),
    ((5, ((0, 0, 0), (0, -3, 1), (4, -6, 1),)), (5, ((0, 0, 0), (4, -3, 0), (4, -6, 1),)), (11, ((0, 0, 0), (4, 0, 0), (4, 2, 1),)), (11, ((0, 0, 0), (0, 1, 1), (4, 2, 1),)),),
    ((3, ((0, 0, 0), (3, 0, 0), (3, 1, 1), (5, 2, 1),)), (2, ((0, 0, 0), (2, 0, 0), (2, 1, 1), (5, 2, 1),)), (8, ((0, 0, 0), (5, 0, 0), (5, 2, 1),)), (9, ((0, 0, 0), (0, 1, 1), (5, 2, 1),)), (5, ((0, 0, 0), (0, -3, 1), (5, -6, 1),)), (5, ((0, 0, 0), (3, -3, 0), (5, -6, 1),)),),
    ((11, ((0, 0, 0), (1, 0, 0), (1, 1, 1), (6, 2, 1),)), (11, ((0, 0, 0), (5, 1, 0), (5, 2, 1), (6, 2, 1),)), (10, ((0, 0, 0), (5, -3, 0), (6, -6, 1),)),),
    ((11, ((0, 0, 0), (5, -3, 0), (7, -6, 1),)), (21, ((0, 0, 0), (7, 2, 1),)),),
    ((12, ((0, 0, 0), (2, -3, 0), (0, -5, 0),)), (20, ((0, 0, 0), (0, 3, 0),)),),
    ((5, ((0, 0, 0), (4, 0, 0), (4, 1, 1), (1, 3, 1),)), (5, ((0, 0, 0), (5, 0, 0), (5, 1, 1), (1, 3, 1),)), (5, ((0, 0, 0), (0, 1, 1), (1, 3, 1),)), (5, ((0, 0, 0), (2, 1, 0), (1, 3, 1),)), (12, ((0, 0, 0), (2, -3, 0), (1, -5, 1),)),),
    ((6, ((0, 0, 0), (5, -3, 0), (5, -5, 1), (2, -5, 1),)), (9, ((0, 0, 0), (5, 0, 0), (5, 1, 1), (2, 3, 1),)), (5, ((0, 0, 0), (0, 1, 1), (2, 3, 1),)), (5, ((0, 0, 0), (2, 1, 0), (2, 3, 1),)), (3, ((0, 0, 0), (0, -3, 1), (2, -5, 1),)), (4, ((0, 0, 0), (2, -3, 0), (2, -5, 1),)),),
    ((3, ((0, 0, 0), (6, 0, 0), (6, 1, 1), (3, 3, 1),)), (8, ((0, 0, 0), (0, 1, 1), (3, 3, 1),)), (8, ((0, 0, 0), (3, 1, 0), (3, 3, 1),)), (13, ((0, 0, 0), (3, -3, 0), (3, -5, 1),)),),
    ((9, ((0, 0, 0), (4, 1, 0), (4, 3, 1),)), (9, ((0, 0, 0), (0, 1, 1), (4, 3, 1),)), (7, ((0, 0, 0), (0, -3, 1), (4, -5, 1),)), (7, ((0, 0, 0), (4, -3, 0), (4, -5, 1),)),),
    ((3, ((0, 0, 0), (2, -3, 0), (2, -5, 1), (5, -5, 1),)), (6, ((0, 0, 0), (0, -3, 1), (5, -5, 1),)), (11, ((0, 0, 0), (0, 1, 1), (5, 3, 1),)), (6, ((0, 0, 0), (5, 1, 0), (5, 3, 1),)), (6, ((0, 0, 0), (5, -3, 0), (5, -5, 1),)),),
    ((7, ((0, 0, 0), (5, -3, 0), (5, -5, 1), (6, -5, 1),)), (9, ((0, 0, 0), (1, 0, 0), (1, 1, 1), (6, 3, 1),)), (8, ((0, 0, 0), (5, 1, 0), (5, 3, 1), (6, 3, 1),)), (8, ((0, 0, 0), (1, -2, 0), (1, -5, 1), (6, -5, 1),)),),
    ((17, ((0, 0, 0), (0, 1, 1), (7, 3, 1),)), (15, ((0, 0, 0), (2, -3, 0), (7, -5, 1),)),),
    ((16, ((0, 0, 0), (2, -3, 0), (0, -4, 0),)), (16, ((0, 0, 0), (2, 1, 0), (0, 4, 0),)),),
    ((17, ((0, 0, 0), (6, -1, 1), (1, -4, 1),)), (15, ((0, 0, 0), (6, 1, 1), (1, 4, 1),)),),
    ((3, ((0, 0, 0), (2, -2, 0), (4, -4, 1), (2, -4, 1),)), (10, ((0, 0, 0), (5, 0, 0), (5, 1, 1), (2, 4, 1),)), (6, ((0, 0, 0), (7, -3, 1), (2, -4, 1),)), (8, ((0, 0, 0), (5, -2, 0), (2, -4, 1),)), (5, ((0, 0, 0), (1, 3, 0), (2, 4, 1),)),),
    ((3, ((0, 0, 0), (5, 0, 0), (5, 1, 1), (3, 4, 1),)), (6, ((0, 0, 0), (0, 1, 1), (3, 4, 1),)), (6, ((0, 0, 0), (3, 2, 0), (3, 4, 1),)), (10, ((0, 0, 0), (3, -2, 0), (3, -4, 1),)), (7, ((0, 0, 0), (0, -3, 1), (3, -4, 1),)),),
    ((7, ((0, 0, 0), (0, 1, 1), (4, 4, 1),)), (7, ((0, 0, 0), (4, 2, 0), (4, 4, 1),)), (9, ((0, 0, 0), (4, -2, 0), (4, -4, 1),)), (9, ((0, 0, 0), (0, -3, 1), (4, -4, 1),)),),
    ((3, ((0, 0, 0), (2, -2, 0), (2, -4, 1), (5, -4, 1),)), (8, ((0, 0, 0), (5, -2, 0), (5, -4, 1),)), (8, ((0, 0, 0), (0, -3, 1), (5, -4, 1),)), (13, ((0, 0, 0), (5, 2, 0), (5, 4, 1),)),),
    ((11, ((0, 0, 0), (1, -2, 0), (1, -4, 1), (6, -4, 1),)), (8, ((0, 0, 0), (5, -3, 0), (6, -4, 1),)), (13, ((0, 0, 0), (7, 2, 0), (6, 4, 1),)),),
    ((6, ((0, 0, 0), (6, -2, 0), (4, -3, 1), (7, -4, 1),)), (7, ((0, 0, 0), (1, -3, 1), (7, -4, 1),)), (7, ((0, 0, 0), (5, -2, 0), (7, -4, 1),)), (12, ((0, 0, 0), (5, 1, 1), (7, 4, 1),)),),
    ((12, ((0, 0, 0), (2, 2, 0), (0, 5, 0),)), (20, ((0, 0, 0), (0, -3, 0),)),),
    ((11, ((0, 0, 0), (0, 2, 1), (1, 5, 1),)), (21, ((0, 0, 0), (1, -3, 1),)),),
    ((11, ((0, 0, 0), (3, -1, 0), (3, -3, 1), (2, -3, 1),)), (5, ((0, 0, 0), (3, 3, 0), (3, 4, 1), (2, 5, 1),)), (10, ((0, 0, 0), (7, -1, 0), (7, -3, 1), (2, -3, 1),)), (6, ((0, 0, 0), (7, 0, 0), (7, 2, 1), (2, 5, 1),)),),
    ((11, ((0, 0, 0), (0, -3, 1), (3, -3, 1),)), (10, ((0, 0, 0), (0, 2, 1), (3, 5, 1),)), (11, ((0, 0, 0), (3, -1, 0), (3, -3, 1),)),),
    ((5, ((0, 0, 0), (4, 3, 0), (4, 5, 1),)), (5, ((0, 0, 0), (0, 2, 1), (4, 5, 1),)), (11, ((0, 0, 0), (0, -3, 1), (4, -3, 1),)), (11, ((0, 0, 0), (4, -1, 0), (4, -3, 1),)),),
    ((5, ((0, 0, 0), (3, -1, 0), (3, -3, 1), (5, -3, 1),)), (9, ((0, 0, 0), (0, -3, 1), (5, -3, 1),)), (9, ((0, 0, 0), (5, -1, 0), (5, -3, 1),)), (9, ((0, 0, 0), (0, 2, 1), (5, 5, 1),)),),
    ((15, ((0, 0, 0), (5, 0, 0), (5, -3, 1), (6, -3, 1),)), (8, ((0, 0, 0), (0, -3, 1), (6, -3, 1),)), (9, ((0, 0, 0), (4, 3, 0), (6, 5, 1),)),),
    ((8, ((0, 0, 0), (3, -1, 0), (3, -3, 1), (7, -3, 1),)), (8, ((0, 0, 0), (6, 0, 0), (4, -1, 1), (7, -3, 1),)), (8, ((0, 0, 0), (1, 2, 1), (7, 5, 1),)), (8, ((0, 0, 0), (7, -3, 1),)),),
    ((8, ((0, 0, 0), (2, 3, 0), (0, 6, 0),)), (24, ((0, 0, 0), (0, -2, 0),)),),
    ((7, ((0, 0, 0), (0, 2, 1), (3, 3, 1), (1, 6, 1),)), (25, ((0, 0, 0), (1, -2, 1),)),),
    ((6, ((0, 0, 0), (2, -1, 0), (4, -2, 1), (2, -2, 1),)), (2, ((0, 0, 0), (2, 1, 0), (4, 3, 1), (2, 6, 1),)), (6, ((0, 0, 0), (6, 0, 0), (6, -2, 1), (2, -2, 1),)), (5, ((0, 0, 0), (7, 1, 0), (7, 3, 1), (2, 6, 1),)), (7, ((0, 0, 0), (0, -2, 1), (2, -2, 1),)), (6, ((0, 0, 0), (4, -1, 0), (2, -2, 1),)),),
    ((3, ((0, 0, 0), (5, 0, 0), (5, -2, 1), (3, -2, 1),)), (3, ((0, 0, 0), (6, 0, 0), (6, -2, 1), (3, -2, 1),)), (6, ((0, 0, 0), (0, 1, 0), (3, 4, 0), (3, 6, 1),)), (10, ((0, 0, 0), (3, 0, 0), (3, -2, 1),)), (10, ((0, 0, 0), (0, -2, 1), (3, -2, 1),)),),
    ((3, ((0, 0, 0), (0, 1, 1), (6, 3, 1), (4, 6, 1),)), (3, ((0, 0, 0), (6, 1, 0), (4, 4, 0), (4, 6, 1),)), (13, ((0, 0, 0), (4, 0, 0), (4, -2, 1),)), (13, ((0, 0, 0), (0, -2, 1), (4, -2, 1),)),),
    ((4, ((0, 0, 0), (2, 0, 0), (2, -2, 1), (5, -2, 1),)), (3, ((0, 0, 0), (3, 0, 0), (3, -2, 1), (5, -2, 1),)), (5, ((0, 0, 0), (6, 1, 0), (5, 4, 0), (5, 6, 1),)), (10, ((0, 0, 0), (5, 0, 0), (5, -2, 1),)), (10, ((0, 0, 0), (0, -2, 1), (5, -2, 1),)),),
    ((5, ((0, 0, 0), (7, 1, 0), (7, 3, 1), (6, 6, 1),)), (6, ((0, 0, 0), (2, 0, 0), (2, -2, 1), (6, -2, 1),)), (5, ((0, 0, 0), (4, 0, 0), (4, -2, 1), (6, -2, 1),)), (8, ((0, 0, 0), (0, -2, 1), (6, -2, 1),)), (8, ((0, 0, 0), (6, 0, 0), (6, -2, 1),)),),
    ((4, ((0, 0, 0), (0, 1, 0), (6, 4, 0), (7, 6, 1),)), (7, ((0, 0, 0), (3, 0, 0), (3, -2, 1), (7, -2, 1),)), (7, ((0, 0, 0), (5, 0, 0), (5, -2, 1), (7, -2, 1),)), (7, ((0, 0, 0), (7, 0, 0), (7, -2, 1),)), (7, ((0, 0, 0), (0, -2, 1), (7, -2, 1),)),),
    ((4, ((0, 0, 0), (0, 1, 0), (3, 4, 0), (0, 7, 0),)), (28, ((0, 0, 0), (0, -1, 0),)),),
    ((3, ((0, 0, 0), (0, 1, 1), (0, 4, 1), (1, 7, 1),)), (29, ((0, 0, 0), (1, -1, 1),)),),
    ((3, ((0, 0, 0), (0, 2, 0), (2, 5, 0), (2, 7, 1),)), (3, ((0, 0, 0), (6, -1, 1), (4, -1, 1), (2, -1, 1),)), (3, ((0, 0, 0), (6, 0, 0), (4, -1, 1), (2, -1, 1),)), (6, ((0, 0, 0), (3, 0, 0), (2, -1, 1),)), (17, ((0, 0, 0), (1, -1, 1), (2, -1, 1),)),),
    ((3, ((0, 0, 0), (6, 2, 0), (4, 5, 0), (3, 7, 1),)), (29, ((0, 0, 0), (3, -1, 1),)),),
    ((32, ((0, 0, 0), (4, -1, 1),)),),
    ((5, ((0, 0, 0), (2, 0, 0), (4, -1, 1), (5, -1, 1),)), (3, ((0, 0, 0), (0, 1, 1), (0, 4, 1), (5, 7, 1),)), (24, ((0, 0, 0), (5, -1, 1),)),),
    ((8, ((0, 0, 0), (2, 0, 0), (4, -1, 1), (6, -1, 1),)), (24, ((0, 0, 0), (6, -1, 1),)),),
    ((32, ((0, 0, 0), (7, -1, 1),)),),
)


def aligned(row):
    return row if isinstance(row, int) else pl.multiple_of(row, 16)


def wrap(x):
    return jnp.where(x >= 8, x - 8, x)


def hop(at, start, end, turn):
    (e0, b0, k0), (e1, b1, k1) = start, end
    source = wrap(at[1] + (-e0) % 8)
    z = wrap(at[0] + (b1 - b0) % 8)
    if k1 != k0:
        z = jnp.where(source >= 8 - turn, wrap(at[0] + (b1 - b0 + k1 - k0) % 8), z)
    return z * 8 + wrap(source + e1 % 8)


def handoff(pages, offset):
    turn = offset % 8
    rows = pages.shape[0]
    paths = []
    row = 0
    for units, states in ROUTES[offset - 1]:
        size = units * rows // (UNITS * CHUNKS)
        paths.append((row, size, states))
        row += size * CHUNKS
    legs = {}
    for p, (_, _, states) in enumerate(paths):
        for i in range(len(states) - 1):
            legs[p, i] = len(legs)
    depth = max(len(states) for _, _, states in paths) - 1
    moves = sorted({m for _, _, states in paths for m in zip(states, states[1:])})

    inner = {}
    for p, i in legs:
        if (p, i + 1) in legs:
            inner[p, i] = len(inner) * CHUNKS
    sent = sum(paths[p][1] * CHUNKS for p, _ in legs)
    held = max(sent, depth * rows)

    def kernel(src, dst, relay, send_sem, last_sem, inner_sem):
        me = lax.axis_index("dp")
        column = lax.axis_index("tensor")
        at = (lax.div(me, 8), lax.rem(me, 8))
        barrier = pltpu.get_barrier_semaphore()
        for start, end in moves:
            pl.semaphore_signal(
                barrier, inc=1, device_id=(hop(at, end, start, turn), column), device_id_type=MESH
            )
        to = {m: hop(at, *m, turn) for m in moves}
        pl.semaphore_wait(barrier, len(moves))

        def copy(p, i, j):
            row0, size, states = paths[p]
            span = pl.ds(aligned(row0 + j * size), size)
            before = pl.ds(aligned((i - 1) * rows + row0 + j * size), size)
            after = pl.ds(aligned(i * rows + row0 + j * size), size)
            return pltpu.make_async_remote_copy(
                src_ref=src.at[span] if i == 0 else relay.at[before],
                dst_ref=relay.at[after] if (p, i) in inner else dst.at[span],
                send_sem=send_sem,
                recv_sem=inner_sem.at[inner[p, i] + j] if (p, i) in inner else last_sem,
                device_id=(to[states[i], states[i + 1]], column),
                device_id_type=MESH,
            )

        def first(j):
            for p in range(len(paths)):
                copy(p, 0, j).start()

        def onward(i, j):
            for p in range(len(paths)):
                if (p, i) in legs:
                    copy(p, i - 1, j).wait_recv()
                    copy(p, i, j).start()

        if CHUNKS == 1:
            first(0)
            for i in range(1, depth):
                onward(i, 0)
        else:
            pl.loop(0, CHUNKS)(first)
        if CHUNKS > 1 and depth > 1:

            @pl.loop(0, CHUNKS + depth - 2)
            def _(step):
                for i in range(1, depth):
                    j = step - (i - 1)
                    pl.when((j >= 0) & (j < CHUNKS))(lambda i=i, j=j: onward(i, j))

        pltpu.make_async_copy(dst, dst, last_sem).wait()
        everything = relay.at[pl.ds(0, sent)]
        pltpu.make_async_copy(everything, everything, send_sem).wait()

    return pl.pallas_call(
        kernel,
        out_shape=jax.ShapeDtypeStruct(pages.shape, pages.dtype),
        in_specs=[pl.BlockSpec(memory_space=pl.ANY)],
        out_specs=pl.BlockSpec(memory_space=pl.ANY),
        scratch_shapes=[
            pltpu.VMEM((held, pages.shape[1]), pages.dtype),
            pltpu.SemaphoreType.DMA,
            pltpu.SemaphoreType.DMA,
            pltpu.SemaphoreType.DMA((max(len(inner), 1) * CHUNKS,)),
        ],
        compiler_params=pltpu.CompilerParams(
            collective_id=offset - 1, has_side_effects=True, vmem_limit_bytes=32 << 20
        ),
        name=f"handoff{offset}",
    )(pages)


def attend(moved, resident, queries, page_dest, page_table, cross_len):
    cap, page, width = moved.shape
    n_res = resident.shape[0]
    n_slots = n_res + cap
    requests = queries.shape[0]
    heads = width // (2 * HEAD_DIM)
    groups = page_dest.shape[0] // cap

    def kernel(dest, length, moved, resident, queries, table, arrived, context, pool, scores, in_sem, out_sem):
        offset = dest[0] // cap
        maker = (lax.axis_index("dp") - offset + groups) % groups

        def fetch(s):
            src = resident.at[s] if s < n_res else moved.at[s - n_res]
            return pltpu.make_async_copy(src, pool.at[s], in_sem.at[s])

        def slot(q):
            return dest[maker * cap + q] % cap

        def place(q):
            return pltpu.make_async_copy(pool.at[n_res + q], arrived.at[slot(q)], out_sem.at[q])

        for s in range(n_slots):
            fetch(s).start()
        row = lax.broadcasted_iota(jnp.int32, table.shape, 0)
        limit = jnp.zeros(table.shape, jnp.int32)
        for r in range(requests):
            limit = jnp.where(row == r, length[r], limit)
        within = lax.broadcasted_iota(jnp.int32, table.shape, 1) < limit
        entries = jnp.where(within, table[...], -1)
        for s in range(n_slots):
            fetch(s).wait()
            if s >= n_res:
                place(s - n_res).start()
            where = s if s < n_res else n_res + slot(s - n_res)
            live = jnp.max((entries == where).astype(jnp.int32), axis=1, keepdims=True) > 0
            for h in range(heads):
                keys = pool[s, :, 2 * h * HEAD_DIM : (2 * h + 1) * HEAD_DIM]
                part = lax.dot_general(
                    queries[:, h * HEAD_DIM : (h + 1) * HEAD_DIM],
                    keys,
                    (((1,), (1,)), ((), ())),
                    preferred_element_type=jnp.float32,
                )
                scores[h, :, s * page : (s + 1) * page] = jnp.where(live, part, -jnp.inf)
        for h in range(heads):
            s = scores[h]
            prob = jnp.exp(s - jnp.max(s, axis=1, keepdims=True))
            total = jnp.sum(prob, axis=1, keepdims=True)
            weights = prob.astype(jnp.bfloat16)
            values = pool[:, :, (2 * h + 1) * HEAD_DIM : (2 * h + 2) * HEAD_DIM]
            summed = jnp.dot(
                weights, values.reshape(n_slots * page, HEAD_DIM), preferred_element_type=jnp.float32
            )
            context[:, h * HEAD_DIM : (h + 1) * HEAD_DIM] = (summed / total).astype(context.dtype)
        for q in range(cap):
            place(q).wait()

    vmem = pl.BlockSpec(memory_space=pltpu.VMEM)
    hbm = pl.BlockSpec(memory_space=pl.ANY)
    return pl.pallas_call(
        kernel,
        grid_spec=pltpu.PrefetchScalarGridSpec(
            num_scalar_prefetch=2,
            grid=(),
            in_specs=[hbm, hbm, vmem, vmem],
            out_specs=[hbm, vmem],
            scratch_shapes=[
                pltpu.VMEM((n_slots, page, width), moved.dtype),
                pltpu.VMEM((heads, requests, n_slots * page), jnp.float32),
                pltpu.SemaphoreType.DMA((n_slots,)),
                pltpu.SemaphoreType.DMA((cap,)),
            ],
        ),
        out_shape=[
            jax.ShapeDtypeStruct(moved.shape, moved.dtype),
            jax.ShapeDtypeStruct(queries.shape, queries.dtype),
        ],
        compiler_params=pltpu.CompilerParams(vmem_limit_bytes=60 << 20),
        name="attend",
    )(page_dest, cross_len, moved, resident, queries, page_table)


def local(new_pages, page_dest, resident, queries, page_table, cross_len):
    cap, page, width = new_pages.shape
    groups = lax.axis_size("dp")
    offset = lax.shift_right_logical(page_dest[0], cap.bit_length() - 1)
    per_z = 8

    def from_z(a):
        def pick(x):
            first = 1 if a == 0 else 0
            ways = [lambda y, o=a * per_z + r: handoff(y, o) for r in range(first, per_z)]
            return lax.switch((offset & (per_z - 1)) - first, ways, x)

        return pick

    moved = lax.switch(
        lax.shift_right_logical(offset, 3),
        [from_z(a) for a in range(groups // per_z)],
        new_pages.reshape(cap * page, width),
    )
    return tuple(
        attend(moved.reshape(cap, page, width), resident, queries, page_dest, page_table, cross_len)
    )


def solution(mesh):
    return jax.shard_map(
        local,
        mesh=mesh,
        in_specs=(
            P("dp", None, "tensor"),
            P(),
            P("dp", None, "tensor"),
            P("dp", "tensor"),
            P("dp", None),
            P("dp"),
        ),
        out_specs=(P("dp", None, "tensor"), P("dp", "tensor")),
        check_vma=False,
    )
```

```python
import jax
import jax.numpy as jnp
from jax import lax
from jax.experimental import pallas as pl
from jax.experimental.pallas import tpu as pltpu
from jax.sharding import PartitionSpec as P

MESH = pl.DeviceIdType.MESH
HEAD_DIM = 256
CHUNKS = 2
UNITS = 32

ROUTES = (
    ((32, ((0, 0, 0), (1, 0, 1),)),),
    ((8, ((0, 0, 0), (6, 0, 0), (4, 0, 1), (2, 0, 1),)), (24, ((0, 0, 0), (2, 0, 1),)),),
    ((5, ((0, 0, 0), (6, 0, 0), (4, 0, 1), (3, 0, 1),)), (27, ((0, 0, 0), (3, 0, 1),)),),
    ((32, ((0, 0, 0), (4, 0, 1),)),),
    ((2, ((0, 0, 0), (2, -3, 1), (4, -6, 1), (5, -8, 1),)), (3, ((0, 0, 0), (2, 0, 0), (4, 0, 1), (5, 0, 1),)), (27, ((0, 0, 0), (5, 0, 1),)),),
    ((3, ((0, 0, 0), (2, -3, 0), (4, -6, 0), (6, -8, 1),)), (4, ((0, 0, 0), (2, 0, 0), (4, 0, 0), (6, 0, 1),)), (25, ((0, 0, 0), (6, 0, 1),)),),
    ((3, ((0, 0, 0), (0, -3, 1), (6, -5, 1), (7, -8, 1),)), (29, ((0, 0, 0), (7, 0, 1),)),),
    ((4, ((0, 0, 0), (0, -3, 0), (4, -6, 0), (0, -7, 0),)), (28, ((0, 0, 0), (0, 1, 0),)),),
    ((4, ((0, 0, 0), (0, -3, 0), (1, -5, 0), (1, -7, 1),)), (7, ((0, 0, 0), (3, 0, 0), (3, 1, 1), (1, 1, 1),)), (7, ((0, 0, 0), (6, 0, 0), (6, 1, 1), (1, 1, 1),)), (7, ((0, 0, 0), (1, 0, 0), (1, 1, 1),)), (7, ((0, 0, 0), (7, 0, 1), (1, 1, 1),)),),
    ((11, ((0, 0, 0), (5, 0, 0), (5, 1, 1), (2, 1, 1),)), (5, ((0, 0, 0), (0, -3, 0), (0, -6, 1), (2, -7, 1),)), (8, ((0, 0, 0), (0, 1, 1), (2, 1, 1),)), (8, ((0, 0, 0), (2, 0, 0), (2, 1, 1),)),),
    ((5, ((0, 0, 0), (0, -3, 0), (3, -5, 0), (3, -7, 1),)), (4, ((0, 0, 0), (6, 0, 0), (6, 1, 1), (3, 1, 1),)), (3, ((0, 0, 0), (5, 0, 0), (5, 1, 1), (3, 1, 1),)), (10, ((0, 0, 0), (0, 1, 1), (3, 1, 1),)), (10, ((0, 0, 0), (3, 0, 0), (3, 1, 1),)),),
    ((3, ((0, 0, 0), (0, -3, 1), (1, -6, 1), (4, -7, 1),)), (3, ((0, 0, 0), (6, -3, 0), (4, -5, 0), (4, -7, 1),)), (13, ((0, 0, 0), (0, 1, 1), (4, 1, 1),)), (13, ((0, 0, 0), (4, 0, 0), (4, 1, 1),)),),
    ((6, ((0, 0, 0), (6, -3, 0), (6, -6, 1), (5, -7, 1),)), (3, ((0, 0, 0), (2, 0, 0), (2, 1, 1), (5, 1, 1),)), (3, ((0, 0, 0), (3, 0, 0), (3, 1, 1), (5, 1, 1),)), (10, ((0, 0, 0), (0, 1, 1), (5, 1, 1),)), (10, ((0, 0, 0), (5, 0, 0), (5, 1, 1),)),),
    ((6, ((0, 0, 0), (2, 0, 0), (2, 1, 1), (6, 1, 1),)), (2, ((0, 0, 0), (4, -3, 0), (4, -6, 1), (6, -7, 1),)), (5, ((0, 0, 0), (1, -3, 0), (1, -6, 1), (6, -7, 1),)), (6, ((0, 0, 0), (4, 0, 0), (4, 1, 1), (6, 1, 1),)), (7, ((0, 0, 0), (0, 1, 1), (6, 1, 1),)), (6, ((0, 0, 0), (6, 0, 0), (6, 1, 1),)),),
    ((7, ((0, 0, 0), (0, -2, 0), (7, -5, 0), (7, -7, 1),)), (25, ((0, 0, 0), (7, 1, 1),)),),
    ((8, ((0, 0, 0), (2, -3, 0), (0, -6, 0),)), (24, ((0, 0, 0), (0, 2, 0),)),),
    ((8, ((0, 0, 0), (5, 0, 0), (5, 2, 1), (1, 2, 1),)), (8, ((0, 0, 0), (1, 0, 0), (1, 2, 1),)), (8, ((0, 0, 0), (0, -3, 1), (1, -6, 1),)), (8, ((0, 0, 0), (7, 1, 1), (1, 2, 1),)),),
    ((15, ((0, 0, 0), (5, 0, 0), (5, 1, 1), (2, 2, 1),)), (9, ((0, 0, 0), (1, -3, 0), (2, -6, 1),)), (8, ((0, 0, 0), (2, 2, 1),)),),
    ((5, ((0, 0, 0), (6, 0, 0), (6, 1, 1), (3, 2, 1),)), (9, ((0, 0, 0), (0, 1, 1), (3, 2, 1),)), (9, ((0, 0, 0), (3, 0, 0), (3, 2, 1),)), (9, ((0, 0, 0), (3, -3, 0), (3, -6, 1),)),),
    ((5, ((0, 0, 0), (0, -3, 1), (4, -6, 1),)), (5, ((0, 0, 0), (4, -3, 0), (4, -6, 1),)), (11, ((0, 0, 0), (4, 0, 0), (4, 2, 1),)), (11, ((0, 0, 0), (0, 1, 1), (4, 2, 1),)),),
    ((11, ((0, 0, 0), (5, 0, 0), (5, 2, 1),)), (11, ((0, 0, 0), (0, 1, 1), (5, 2, 1),)), (10, ((0, 0, 0), (0, -3, 1), (5, -6, 1),)),),
    ((11, ((0, 0, 0), (1, 0, 0), (1, 1, 1), (6, 2, 1),)), (11, ((0, 0, 0), (5, 0, 0), (5, 2, 1), (6, 2, 1),)), (10, ((0, 0, 0), (5, -3, 0), (6, -6, 1),)),),
    ((11, ((0, 0, 0), (0, -3, 1), (7, -6, 1),)), (21, ((0, 0, 0), (7, 2, 1),)),),
    ((12, ((0, 0, 0), (2, -3, 0), (0, -5, 0),)), (20, ((0, 0, 0), (0, 3, 0),)),),
    ((6, ((0, 0, 0), (2, 1, 0), (4, 1, 1), (1, 3, 1),)), (12, ((0, 0, 0), (0, -3, 1), (1, -5, 1),)), (7, ((0, 0, 0), (3, 1, 0), (1, 3, 1),)), (7, ((0, 0, 0), (5, 0, 1), (1, 3, 1),)),),
    ((6, ((0, 0, 0), (5, -3, 0), (5, -5, 1), (2, -5, 1),)), (9, ((0, 0, 0), (5, 0, 0), (5, 1, 1), (2, 3, 1),)), (5, ((0, 0, 0), (0, 1, 1), (2, 3, 1),)), (5, ((0, 0, 0), (2, 1, 0), (2, 3, 1),)), (4, ((0, 0, 0), (0, -3, 1), (2, -5, 1),)), (3, ((0, 0, 0), (2, -3, 0), (2, -5, 1),)),),
    ((3, ((0, 0, 0), (6, 0, 0), (6, 1, 1), (3, 3, 1),)), (8, ((0, 0, 0), (0, 1, 1), (3, 3, 1),)), (8, ((0, 0, 0), (3, 1, 0), (3, 3, 1),)), (13, ((0, 0, 0), (3, -3, 0), (3, -5, 1),)),),
    ((9, ((0, 0, 0), (4, 1, 0), (4, 3, 1),)), (9, ((0, 0, 0), (0, 1, 1), (4, 3, 1),)), (7, ((0, 0, 0), (0, -3, 1), (4, -5, 1),)), (7, ((0, 0, 0), (4, -3, 0), (4, -5, 1),)),),
    ((3, ((0, 0, 0), (3, -3, 0), (3, -5, 1), (5, -5, 1),)), (11, ((0, 0, 0), (0, 1, 1), (5, 3, 1),)), (6, ((0, 0, 0), (5, 1, 0), (5, 3, 1),)), (6, ((0, 0, 0), (5, -3, 0), (5, -5, 1),)), (6, ((0, 0, 0), (0, -3, 1), (5, -5, 1),)),),
    ((10, ((0, 0, 0), (3, -3, 0), (3, -5, 1), (6, -5, 1),)), (11, ((0, 0, 0), (1, 0, 0), (1, 2, 1), (6, 3, 1),)), (6, ((0, 0, 0), (5, 0, 0), (5, 1, 1), (6, 3, 1),)), (5, ((0, 0, 0), (0, -3, 1), (6, -5, 1),)),),
    ((17, ((0, 0, 0), (0, 1, 1), (7, 3, 1),)), (15, ((0, 0, 0), (4, -3, 0), (7, -5, 1),)),),
    ((16, ((0, 0, 0), (2, -3, 0), (0, -4, 0),)), (16, ((0, 0, 0), (2, 1, 0), (0, 4, 0),)),),
    ((15, ((0, 0, 0), (2, 2, 0), (1, 4, 1),)), (17, ((0, 0, 0), (2, -2, 0), (1, -4, 1),)),),
    ((15, ((0, 0, 0), (7, 3, 0), (7, 4, 1), (2, 4, 1),)), (17, ((0, 0, 0), (6, -2, 0), (2, -4, 1),)),),
    ((3, ((0, 0, 0), (6, -2, 0), (6, -4, 1), (3, -4, 1),)), (9, ((0, 0, 0), (0, 1, 1), (3, 4, 1),)), (5, ((0, 0, 0), (3, 2, 0), (3, 4, 1),)), (9, ((0, 0, 0), (3, -2, 0), (3, -4, 1),)), (6, ((0, 0, 0), (0, -3, 1), (3, -4, 1),)),),
    ((7, ((0, 0, 0), (0, 1, 1), (4, 4, 1),)), (7, ((0, 0, 0), (4, 2, 0), (4, 4, 1),)), (9, ((0, 0, 0), (4, -2, 0), (4, -4, 1),)), (9, ((0, 0, 0), (0, -3, 1), (4, -4, 1),)),),
    ((3, ((0, 0, 0), (2, -2, 0), (2, -4, 1), (5, -4, 1),)), (8, ((0, 0, 0), (5, -2, 0), (5, -4, 1),)), (8, ((0, 0, 0), (0, -3, 1), (5, -4, 1),)), (13, ((0, 0, 0), (5, 2, 0), (5, 4, 1),)),),
    ((11, ((0, 0, 0), (1, -2, 0), (1, -4, 1), (6, -4, 1),)), (8, ((0, 0, 0), (5, -3, 0), (6, -4, 1),)), (13, ((0, 0, 0), (2, 3, 0), (6, 4, 1),)),),
    ((6, ((0, 0, 0), (6, -3, 0), (4, -4, 1), (7, -4, 1),)), (7, ((0, 0, 0), (1, -3, 1), (7, -4, 1),)), (7, ((0, 0, 0), (3, -1, 0), (7, -4, 1),)), (12, ((0, 0, 0), (2, 2, 1), (7, 4, 1),)),),
    ((12, ((0, 0, 0), (2, 2, 0), (0, 5, 0),)), (20, ((0, 0, 0), (0, -3, 0),)),),
    ((11, ((0, 0, 0), (0, 2, 1), (1, 5, 1),)), (21, ((0, 0, 0), (1, -3, 1),)),),
    ((11, ((0, 0, 0), (3, -1, 0), (3, -3, 1), (2, -3, 1),)), (11, ((0, 0, 0), (7, -1, 0), (7, -3, 1), (2, -3, 1),)), (10, ((0, 0, 0), (4, 3, 0), (2, 5, 1),)),),
    ((3, ((0, 0, 0), (5, -1, 0), (5, -3, 1), (3, -3, 1),)), (2, ((0, 0, 0), (6, -1, 0), (6, -3, 1), (3, -3, 1),)), (9, ((0, 0, 0), (0, -3, 1), (3, -3, 1),)), (4, ((0, 0, 0), (3, 3, 0), (3, 5, 1),)), (8, ((0, 0, 0), (3, -1, 0), (3, -3, 1),)), (6, ((0, 0, 0), (1, 2, 1), (3, 5, 1),)),),
    ((5, ((0, 0, 0), (4, 3, 0), (4, 5, 1),)), (5, ((0, 0, 0), (0, 2, 1), (4, 5, 1),)), (11, ((0, 0, 0), (0, -3, 1), (4, -3, 1),)), (11, ((0, 0, 0), (4, -1, 0), (4, -3, 1),)),),
    ((5, ((0, 0, 0), (3, -1, 0), (3, -3, 1), (5, -3, 1),)), (9, ((0, 0, 0), (0, -3, 1), (5, -3, 1),)), (9, ((0, 0, 0), (5, -1, 0), (5, -3, 1),)), (9, ((0, 0, 0), (1, 2, 1), (5, 5, 1),)),),
    ((15, ((0, 0, 0), (3, -1, 0), (3, -3, 1), (6, -3, 1),)), (9, ((0, 0, 0), (4, 3, 0), (6, 5, 1),)), (8, ((0, 0, 0), (6, -3, 1),)),),
    ((6, ((0, 0, 0), (3, -1, 0), (3, -3, 1), (7, -3, 1),)), (6, ((0, 0, 0), (6, -2, 0), (4, -3, 1), (7, -3, 1),)), (8, ((0, 0, 0), (6, 3, 0), (7, 5, 1),)), (6, ((0, 0, 0), (1, -3, 1), (7, -3, 1),)), (6, ((0, 0, 0), (5, -2, 0), (7, -3, 1),)),),
    ((8, ((0, 0, 0), (2, 3, 0), (0, 6, 0),)), (24, ((0, 0, 0), (0, -2, 0),)),),
    ((7, ((0, 0, 0), (2, 1, 1), (4, 3, 1), (1, 6, 1),)), (25, ((0, 0, 0), (1, -2, 1),)),),
    ((5, ((0, 0, 0), (7, 1, 0), (7, 3, 1), (2, 6, 1),)), (2, ((0, 0, 0), (0, 1, 0), (3, 4, 0), (2, 6, 1),)), (6, ((0, 0, 0), (2, -1, 0), (4, -2, 1), (2, -2, 1),)), (6, ((0, 0, 0), (6, 0, 0), (6, -2, 1), (2, -2, 1),)), (7, ((0, 0, 0), (0, -2, 1), (2, -2, 1),)), (6, ((0, 0, 0), (4, -1, 0), (2, -2, 1),)),),
    ((6, ((0, 0, 0), (2, 1, 0), (2, 3, 1), (3, 6, 1),)), (3, ((0, 0, 0), (5, 0, 0), (5, -2, 1), (3, -2, 1),)), (3, ((0, 0, 0), (6, 0, 0), (6, -2, 1), (3, -2, 1),)), (10, ((0, 0, 0), (0, -2, 1), (3, -2, 1),)), (10, ((0, 0, 0), (3, 0, 0), (3, -2, 1),)),),
    ((3, ((0, 0, 0), (0, 1, 1), (2, 3, 1), (4, 6, 1),)), (3, ((0, 0, 0), (6, 1, 0), (4, 4, 0), (4, 6, 1),)), (13, ((0, 0, 0), (4, 0, 0), (4, -2, 1),)), (13, ((0, 0, 0), (0, -2, 1), (4, -2, 1),)),),
    ((4, ((0, 0, 0), (2, 0, 0), (2, -2, 1), (5, -2, 1),)), (3, ((0, 0, 0), (3, 0, 0), (3, -2, 1), (5, -2, 1),)), (5, ((0, 0, 0), (6, 1, 0), (5, 4, 0), (5, 6, 1),)), (10, ((0, 0, 0), (5, 0, 0), (5, -2, 1),)), (10, ((0, 0, 0), (0, -2, 1), (5, -2, 1),)),),
    ((9, ((0, 0, 0), (2, 0, 0), (2, -2, 1), (6, -2, 1),)), (5, ((0, 0, 0), (0, 2, 0), (0, 4, 0), (6, 6, 1),)), (9, ((0, 0, 0), (0, -2, 1), (6, -2, 1),)), (9, ((0, 0, 0), (6, 0, 0), (6, -2, 1),)),),
    ((7, ((0, 0, 0), (3, 0, 0), (3, -2, 1), (7, -2, 1),)), (7, ((0, 0, 0), (5, 0, 0), (5, -2, 1), (7, -2, 1),)), (4, ((0, 0, 0), (0, 1, 0), (0, 3, 1), (7, 6, 1),)), (7, ((0, 0, 0), (7, 0, 0), (7, -2, 1),)), (7, ((0, 0, 0), (0, -2, 1), (7, -2, 1),)),),
    ((4, ((0, 0, 0), (0, 1, 0), (3, 4, 0), (0, 7, 0),)), (28, ((0, 0, 0), (0, -1, 0),)),),
    ((3, ((0, 0, 0), (0, 2, 0), (1, 4, 1), (1, 7, 1),)), (29, ((0, 0, 0), (1, -1, 1),)),),
    ((3, ((0, 0, 0), (6, 2, 0), (4, 5, 0), (2, 7, 1),)), (4, ((0, 0, 0), (6, 0, 0), (4, -1, 1), (2, -1, 1),)), (25, ((0, 0, 0), (2, -1, 1),)),),
    ((3, ((0, 0, 0), (6, 0, 0), (4, 0, 0), (3, -1, 1),)), (2, ((0, 0, 0), (6, 2, 0), (4, 4, 1), (3, 7, 1),)), (27, ((0, 0, 0), (3, -1, 1),)),),
    ((32, ((0, 0, 0), (4, -1, 1),)),),
    ((5, ((0, 0, 0), (2, 0, 0), (4, -1, 1), (5, -1, 1),)), (27, ((0, 0, 0), (5, -1, 1),)),),
    ((8, ((0, 0, 0), (2, 0, 0), (4, -1, 1), (6, -1, 1),)), (24, ((0, 0, 0), (6, -1, 1),)),),
    ((32, ((0, 0, 0), (7, -1, 1),)),),
)


def aligned(row):
    return row if isinstance(row, int) else pl.multiple_of(row, 16)


def wrap(x):
    return jnp.where(x >= 8, x - 8, x)


def hop(at, start, end, turn):
    (e0, b0, k0), (e1, b1, k1) = start, end
    source = wrap(at[1] + (-e0) % 8)
    z = wrap(at[0] + (b1 - b0) % 8)
    if k1 != k0:
        z = jnp.where(source >= 8 - turn, wrap(at[0] + (b1 - b0 + k1 - k0) % 8), z)
    return z * 8 + wrap(source + e1 % 8)


def handoff(pages, offset):
    turn = offset % 8
    rows = pages.shape[0]
    paths = []
    row = 0
    for units, states in ROUTES[offset - 1]:
        size = units * rows // (UNITS * CHUNKS)
        paths.append((row, size, states))
        row += size * CHUNKS
    legs = {}
    for p, (_, _, states) in enumerate(paths):
        for i in range(len(states) - 1):
            legs[p, i] = len(legs)
    depth = max(len(states) for _, _, states in paths) - 1
    moves = sorted({m for _, _, states in paths for m in zip(states, states[1:])})

    inner = {}
    for p, i in legs:
        if (p, i + 1) in legs:
            inner[p, i] = len(inner) * CHUNKS
    sent = sum(paths[p][1] * CHUNKS for p, _ in legs)
    held = max(sent, depth * rows)

    def kernel(src, dst, relay, send_sem, last_sem, inner_sem):
        me = lax.axis_index("dp")
        column = lax.axis_index("tensor")
        at = (lax.div(me, 8), lax.rem(me, 8))
        barrier = pltpu.get_barrier_semaphore()
        for start, end in moves:
            pl.semaphore_signal(
                barrier, inc=1, device_id=(hop(at, end, start, turn), column), device_id_type=MESH
            )
        to = {m: hop(at, *m, turn) for m in moves}
        pl.semaphore_wait(barrier, len(moves))

        def copy(p, i, j):
            row0, size, states = paths[p]
            span = pl.ds(aligned(row0 + j * size), size)
            before = pl.ds(aligned((i - 1) * rows + row0 + j * size), size)
            after = pl.ds(aligned(i * rows + row0 + j * size), size)
            return pltpu.make_async_remote_copy(
                src_ref=src.at[span] if i == 0 else relay.at[before],
                dst_ref=relay.at[after] if (p, i) in inner else dst.at[span],
                send_sem=send_sem,
                recv_sem=inner_sem.at[inner[p, i] + j] if (p, i) in inner else last_sem,
                device_id=(to[states[i], states[i + 1]], column),
                device_id_type=MESH,
            )

        def first(j):
            for p in range(len(paths)):
                copy(p, 0, j).start()

        def onward(i, j):
            for p in range(len(paths)):
                if (p, i) in legs:
                    copy(p, i - 1, j).wait_recv()
                    copy(p, i, j).start()

        if CHUNKS == 1:
            first(0)
            for i in range(1, depth):
                onward(i, 0)
        else:
            pl.loop(0, CHUNKS)(first)
        if CHUNKS > 1 and depth > 1:

            @pl.loop(0, CHUNKS + depth - 2)
            def _(step):
                for i in range(1, depth):
                    j = step - (i - 1)
                    pl.when((j >= 0) & (j < CHUNKS))(lambda i=i, j=j: onward(i, j))

        pltpu.make_async_copy(dst, dst, last_sem).wait()
        everything = relay.at[pl.ds(0, sent)]
        pltpu.make_async_copy(everything, everything, send_sem).wait()

    return pl.pallas_call(
        kernel,
        out_shape=jax.ShapeDtypeStruct(pages.shape, pages.dtype),
        in_specs=[pl.BlockSpec(memory_space=pl.ANY)],
        out_specs=pl.BlockSpec(memory_space=pl.ANY),
        scratch_shapes=[
            pltpu.VMEM((held, pages.shape[1]), pages.dtype),
            pltpu.SemaphoreType.DMA,
            pltpu.SemaphoreType.DMA,
            pltpu.SemaphoreType.DMA((max(len(inner), 1) * CHUNKS,)),
        ],
        compiler_params=pltpu.CompilerParams(
            collective_id=offset - 1, has_side_effects=True, vmem_limit_bytes=32 << 20
        ),
        name=f"handoff{offset}",
    )(pages)


def attend(moved, resident, queries, page_dest, page_table, cross_len):
    cap, page, width = moved.shape
    n_res = resident.shape[0]
    n_slots = n_res + cap
    requests = queries.shape[0]
    heads = width // (2 * HEAD_DIM)
    groups = page_dest.shape[0] // cap

    def kernel(dest, length, moved, resident, queries, table, arrived, context, pool, scores, in_sem, out_sem):
        offset = dest[0] // cap
        maker = (lax.axis_index("dp") - offset + groups) % groups

        def fetch(s):
            src = resident.at[s] if s < n_res else moved.at[s - n_res]
            return pltpu.make_async_copy(src, pool.at[s], in_sem.at[s])

        def slot(q):
            return dest[maker * cap + q] % cap

        def place(q):
            return pltpu.make_async_copy(pool.at[n_res + q], arrived.at[slot(q)], out_sem.at[q])

        for s in range(n_slots):
            fetch(s).start()
        row = lax.broadcasted_iota(jnp.int32, table.shape, 0)
        limit = jnp.zeros(table.shape, jnp.int32)
        for r in range(requests):
            limit = jnp.where(row == r, length[r], limit)
        within = lax.broadcasted_iota(jnp.int32, table.shape, 1) < limit
        entries = jnp.where(within, table[...], -1)
        for s in range(n_slots):
            fetch(s).wait()
            if s >= n_res:
                place(s - n_res).start()
            where = s if s < n_res else n_res + slot(s - n_res)
            live = jnp.max((entries == where).astype(jnp.int32), axis=1, keepdims=True) > 0
            for h in range(heads):
                keys = pool[s, :, 2 * h * HEAD_DIM : (2 * h + 1) * HEAD_DIM]
                part = lax.dot_general(
                    queries[:, h * HEAD_DIM : (h + 1) * HEAD_DIM],
                    keys,
                    (((1,), (1,)), ((), ())),
                    preferred_element_type=jnp.float32,
                )
                scores[h, :, s * page : (s + 1) * page] = jnp.where(live, part, -jnp.inf)
        for h in range(heads):
            s = scores[h]
            prob = jnp.exp(s - jnp.max(s, axis=1, keepdims=True))
            total = jnp.sum(prob, axis=1, keepdims=True)
            weights = prob.astype(jnp.bfloat16)
            values = pool[:, :, (2 * h + 1) * HEAD_DIM : (2 * h + 2) * HEAD_DIM]
            summed = jnp.dot(
                weights, values.reshape(n_slots * page, HEAD_DIM), preferred_element_type=jnp.float32
            )
            context[:, h * HEAD_DIM : (h + 1) * HEAD_DIM] = (summed / total).astype(context.dtype)
        for q in range(cap):
            place(q).wait()

    vmem = pl.BlockSpec(memory_space=pltpu.VMEM)
    hbm = pl.BlockSpec(memory_space=pl.ANY)
    return pl.pallas_call(
        kernel,
        grid_spec=pltpu.PrefetchScalarGridSpec(
            num_scalar_prefetch=2,
            grid=(),
            in_specs=[hbm, hbm, vmem, vmem],
            out_specs=[hbm, vmem],
            scratch_shapes=[
                pltpu.VMEM((n_slots, page, width), moved.dtype),
                pltpu.VMEM((heads, requests, n_slots * page), jnp.float32),
                pltpu.SemaphoreType.DMA((n_slots,)),
                pltpu.SemaphoreType.DMA((cap,)),
            ],
        ),
        out_shape=[
            jax.ShapeDtypeStruct(moved.shape, moved.dtype),
            jax.ShapeDtypeStruct(queries.shape, queries.dtype),
        ],
        compiler_params=pltpu.CompilerParams(vmem_limit_bytes=60 << 20),
        name="attend",
    )(page_dest, cross_len, moved, resident, queries, page_table)


def local(new_pages, page_dest, resident, queries, page_table, cross_len):
    cap, page, width = new_pages.shape
    groups = lax.axis_size("dp")
    offset = lax.shift_right_logical(page_dest[0], cap.bit_length() - 1)
    per_z = 8

    def from_z(a):
        def pick(x):
            first = 1 if a == 0 else 0
            ways = [lambda y, o=a * per_z + r: handoff(y, o) for r in range(first, per_z)]
            return lax.switch((offset & (per_z - 1)) - first, ways, x)

        return pick

    moved = lax.switch(
        lax.shift_right_logical(offset, 3),
        [from_z(a) for a in range(groups // per_z)],
        new_pages.reshape(cap * page, width),
    )
    return tuple(
        attend(moved.reshape(cap, page, width), resident, queries, page_dest, page_table, cross_len)
    )


def solution(mesh):
    return jax.shard_map(
        local,
        mesh=mesh,
        in_specs=(
            P("dp", None, "tensor"),
            P(),
            P("dp", None, "tensor"),
            P("dp", "tensor"),
            P("dp", None),
            P("dp"),
        ),
        out_specs=(P("dp", None, "tensor"), P("dp", "tensor")),
        check_vma=False,
    )
```
